32 devices in a mesh: dp: 4 (over z), ctx: 2 (over y), fsdp: 4 (over x, core).
Axes of the slice: x: 2, y: 2, z: 4, core: 2. Of those that a mesh axis runs over, the one named last changes fastest.
Arguments:
- tokens: bfloat16 [16, 1024, 2048], P(('dp', 'fsdp'), 'ctx'), may hold values from -6 to 6
- cotangent: bfloat16 [16, 1024, 2048], P(('dp', 'fsdp'), 'ctx'), may hold values from -6 to 6
- positions: int32 [16, 1024], P(('dp', 'fsdp'), 'ctx'), may hold values from 0 to 1023, as said below
- block_map: int32 [4], replicated, may hold values from 0 to 3, as said below
- w_query: bfloat16 [2048, 2048], P(('dp', 'fsdp')), may hold values from -0.125 to 0.125
- w_key: bfloat16 [2048, 1024], P(('dp', 'fsdp')), may hold values from -0.125 to 0.125
- w_value: bfloat16 [2048, 1024], P(('dp', 'fsdp')), may hold values from -0.125 to 0.125
- w_output: bfloat16 [2048, 2048], P(('dp', 'fsdp')), may hold values from -1 to 1
- w_gate: bfloat16 [2048, 6144], P(('dp', 'fsdp')), may hold values from -0.125 to 0.125
- w_up: bfloat16 [2048, 6144], P(('dp', 'fsdp')), may hold values from -0.125 to 0.125
- w_down: bfloat16 [6144, 2048], P(('dp', 'fsdp')), may hold values from -0.078125 to 0.078125
- gain_attn: bfloat16 [2048], P(('dp', 'fsdp')), may hold values from 0.5 to 1.5
- gain_mlp: bfloat16 [2048], P(('dp', 'fsdp')), may hold values from 0.5 to 1.5
- gain_query: bfloat16 [128], P(('dp', 'fsdp')), may hold values from 0.5 to 1.5
- gain_key: bfloat16 [128], P(('dp', 'fsdp')), may hold values from 0.5 to 1.5
Outputs:
- output: bfloat16 [16, 1024, 2048], P(('dp', 'fsdp'), 'ctx')
- grad_tokens: bfloat16 [16, 1024, 2048], P(('dp', 'fsdp'), 'ctx')
- grad_query: float32 [2048, 2048], P(('dp', 'fsdp'))
- grad_key: float32 [2048, 1024], P(('dp', 'fsdp'))
- grad_value: float32 [2048, 1024], P(('dp', 'fsdp'))
- grad_output: float32 [2048, 2048], P(('dp', 'fsdp'))
- grad_gate: float32 [2048, 6144], P(('dp', 'fsdp'))
- grad_up: float32 [2048, 6144], P(('dp', 'fsdp'))
- grad_down: float32 [6144, 2048], P(('dp', 'fsdp'))
- grad_gain_attn: float32 [2048], P(('dp', 'fsdp'))
- grad_gain_mlp: float32 [2048], P(('dp', 'fsdp'))
- grad_gain_query: float32 [128], P(('dp', 'fsdp'))
- grad_gain_key: float32 [128], P(('dp', 'fsdp'))
The draws below stay inside these ranges and needn't reach their ends.
Inputs may be any that keep to these rules, and one draw needn't show every extreme that they name: `block_map`: entries 2c and 2c + 1 are the two blocks held by the c-th device of ctx, a pair b and 3 - b in either order; every block appears once. `positions`: in each sequence's natural token order a position counts up by one from 0, starting again at each document's first token; the first token starts a document; the first sequence is one document; rows are laid out in the order of block_map.
All inputs are finite; a program needn't handle non-finite values.
Results may differ from the reference program's by a relative error of at most 0.02.
Values may be sent and summed in bfloat16 or wider, within the bound.
A program may use at most 512 MiB of HBM per device.

```python
import jax
import jax.numpy as jnp
from jax import lax

D = 2048
HEADS = 16
KV_HEADS = 8
HEAD_DIM = 128
FF = 6144
SEQ = 1024
NSEQ = 16
BLOCKS = 4
BLOCK = 256


def block_table(key):
    order = jax.random.permutation(jax.random.fold_in(key, 11), BLOCKS // 2).astype(jnp.int32)
    flips = jax.random.randint(jax.random.fold_in(key, 12), (BLOCKS // 2,), 0, 2)
    first = jnp.where(flips == 0, order, BLOCKS - 1 - order)
    return jnp.stack([first, BLOCKS - 1 - first], axis=1).reshape(BLOCKS).astype(jnp.int32)


def draw_block_map(key, part):
    return block_table(key)


def draw_positions(key, part):
    table = block_table(key)
    index = jnp.arange(SEQ, dtype=jnp.int32)
    row_index = jnp.arange(NSEQ, dtype=jnp.int32)
    starts = jax.random.randint(jax.random.fold_in(key, 13), (NSEQ, SEQ), 0, SEQ // 4) == 0
    starts = jnp.logical_and(starts, row_index[:, None] != 0)
    starts = jnp.logical_or(starts, index[None, :] == 0)
    begin = lax.cummax(jnp.where(starts, index[None, :], 0), axis=1)
    natural_pos = (index[None, :] - begin).astype(jnp.int32)
    device_index = jnp.repeat(table, BLOCK) * BLOCK + index % BLOCK
    return jnp.take(natural_pos, device_index, axis=1).astype(jnp.int32)


def block_scale(key, shape, cuts, smallest, largest):
    level = 1.0
    for axis_at, blocks in cuts:
        draws = jax.random.uniform(jax.random.fold_in(jax.random.fold_in(key, 6), axis_at), (blocks,), jnp.float32, smallest / len(cuts), largest / len(cuts))
        level = level * jnp.repeat(jnp.exp(draws), shape[axis_at] // blocks).reshape((-1,) + (1,) * (len(shape) - 1 - axis_at))
    return level


def normal_values(key, extent, width, most, shards=(), kind=jnp.bfloat16):
    array = jax.random.normal(key, extent, jnp.float32) * width
    if len(shards) > 0:
        array = block_scale(key, extent, shards, -0.22, 0.18) * array
    return jnp.clip(array, min=-most, max=most).astype(kind)


def setup_inputs(seed: int = 0) -> dict:
    streams_of = jax.random.split(jax.random.key(seed), 16)
    return {
        "tokens": normal_values(streams_of[0], (NSEQ, SEQ, D), 1.0, 6.0, ((0, 16), (1, 2))),
        "cotangent": normal_values(streams_of[1], (NSEQ, SEQ, D), 1.0, 6.0, ((0, 16), (1, 2))),
        "positions": draw_positions(jax.random.fold_in(streams_of[15], 71), 0),
        "block_map": draw_block_map(jax.random.fold_in(streams_of[15], 71), 0),
        "w_query": normal_values(streams_of[4], (D, HEADS * HEAD_DIM), D ** -0.5, 0.125, ((0, 16),)),
        "w_key": normal_values(streams_of[5], (D, KV_HEADS * HEAD_DIM), D ** -0.5, 0.125, ((0, 16),)),
        "w_value": normal_values(streams_of[6], (D, KV_HEADS * HEAD_DIM), D ** -0.5, 0.125, ((0, 16),)),
        "w_output": normal_values(streams_of[7], (HEADS * HEAD_DIM, D), (HEADS * HEAD_DIM * 16 // SEQ) ** -0.5, 1.0, ((0, 16),)),
        "w_gate": normal_values(streams_of[8], (D, FF), D ** -0.5, 0.125, ((0, 16),)),
        "w_up": normal_values(streams_of[9], (D, FF), D ** -0.5, 0.125, ((0, 16),)),
        "w_down": normal_values(streams_of[10], (FF, D), FF ** -0.5, 0.078125, ((0, 16),)),
        "gain_attn": jnp.clip(1.0 + 0.1 * jax.random.normal(streams_of[11], (D,), jnp.float32), 0.5, 1.5).astype(jnp.bfloat16),
        "gain_mlp": jnp.clip(1.0 + 0.1 * jax.random.normal(streams_of[12], (D,), jnp.float32), 0.5, 1.5).astype(jnp.bfloat16),
        "gain_query": jnp.clip(1.0 + 0.1 * jax.random.normal(streams_of[13], (HEAD_DIM,), jnp.float32), 0.5, 1.5).astype(jnp.bfloat16),
        "gain_key": jnp.clip(1.0 + 0.1 * jax.random.normal(streams_of[14], (HEAD_DIM,), jnp.float32), 0.5, 1.5).astype(jnp.bfloat16),
    }


EPS = 1e-06
THETA = 1000000.0

@jax.custom_vjp
def low(v):
    return lax.optimization_barrier(v.astype(jnp.bfloat16)).astype(jnp.float32)

@jax.custom_vjp
def low_back(v):
    return v

def low_keep(v):
    return (low(v), None)

def low_pass(kept, grad):
    return (grad,)

def back_keep(v):
    return (v, None)

def back_low(kept, grad):
    return (low(grad),)
low.defvjp(low_keep, low_pass)
low_back.defvjp(back_keep, back_low)

def product_hi(left, right):
    return jnp.dot(left, right, precision=lax.Precision.HIGHEST)

def rms_scale(values, gain):
    return values * lax.rsqrt(lax.optimization_barrier(jnp.mean(values * values, axis=-1, keepdims=True)) + EPS) * gain

def rope_tables(positions):
    half = HEAD_DIM // 2
    freqs = THETA ** (-(jnp.arange(half, dtype=jnp.float32) * 2.0 / HEAD_DIM))
    angles = positions.astype(jnp.float32)[..., None] * freqs
    return (jnp.cos(angles), jnp.sin(angles))

def rotate(values, cosine, sine):
    half = values.shape[-1] // 2
    first = values[..., :half]
    second = values[..., half:]
    cos_b = cosine[..., None, :]
    sin_b = sine[..., None, :]
    return jnp.concatenate([first * cos_b - second * sin_b, second * cos_b + first * sin_b], axis=-1)

def head_post(linear, gain, cosine, sine, heads, factor):
    shaped = linear.reshape(linear.shape[:-1] + (heads, HEAD_DIM))
    return rotate(rms_scale(shaped, gain), cosine, sine) * factor

def layer(xs, wq, wk, wv, wo, wg, wu, wd, ga, gm, gq, gk, cosine, sine, allowed):
    group = HEADS // KV_HEADS
    h1 = low(rms_scale(xs, ga))
    q_lin = low_back(product_hi(h1, wq))
    k_lin = low_back(product_hi(h1, wk))
    values = low(low_back(product_hi(h1, wv)))
    query = low(head_post(q_lin, gq, cosine, sine, HEADS, HEAD_DIM ** (-0.5)))
    keys = low(head_post(k_lin, gk, cosine, sine, KV_HEADS, 1.0))
    q_groups = jnp.moveaxis(query.reshape(SEQ, KV_HEADS, group, HEAD_DIM), 1, 0)
    k_groups = jnp.moveaxis(keys, 1, 0)
    v_groups = jnp.moveaxis(values.reshape(SEQ, KV_HEADS, HEAD_DIM), 1, 0)

    def one_head(items):
        query_head, key_head, value_head = items
        scores = low_back(jnp.einsum('qgd,kd->gqk', query_head, key_head, precision=lax.Precision.HIGHEST))
        scores = jnp.where(allowed, scores, -1e+30)
        shifted = scores - lax.optimization_barrier(jnp.max(scores, axis=-1, keepdims=True))
        exponent = jnp.exp(shifted)
        probs = low(exponent / lax.optimization_barrier(jnp.sum(exponent, axis=-1, keepdims=True)))
        return jnp.einsum('gqk,kd->qgd', probs, value_head, precision=lax.Precision.HIGHEST)
    attended = lax.map(jax.checkpoint(one_head), (q_groups, k_groups, v_groups))
    attended = low(low_back(jnp.moveaxis(attended, 0, 1).reshape(SEQ, HEADS * HEAD_DIM)))
    x_mid = xs + low_back(product_hi(attended, wo))
    h2 = low(rms_scale(x_mid, gm))
    gate = low_back(product_hi(h2, wg))
    upper = low_back(product_hi(h2, wu))
    hidden = low(gate / (1.0 + jnp.exp(-gate)) * upper)
    return x_mid + product_hi(hidden, wd)

def reference(tokens, cotangent, positions, block_map, w_query, w_key, w_value, w_output, w_gate, w_up, w_down, gain_attn, gain_mlp, gain_query, gain_key):
    natural = jnp.repeat(block_map, BLOCK) * BLOCK + jnp.arange(SEQ, dtype=jnp.int32) % BLOCK
    allowed = natural[None, :] <= natural[:, None]
    weights = tuple((w.astype(jnp.float32) for w in (w_query, w_key, w_value, w_output, w_gate, w_up, w_down, gain_attn, gain_mlp, gain_query, gain_key)))

    def step(totals, items):
        x_seq, d_seq, pos_seq = items
        cosine, sine = rope_tables(pos_seq)

        def forward(x_in, wq, wk, wv, wo, wg, wu, wd, ga, gm, gq, gk):
            return layer(x_in, wq, wk, wv, wo, wg, wu, wd, ga, gm, gq, gk, cosine, sine, allowed)
        result, pullback = jax.vjp(forward, x_seq.astype(jnp.float32), *weights)
        grads = pullback(d_seq.astype(jnp.float32))
        totals = tuple((t + g for t, g in zip(totals, grads[1:])))
        return (totals, (result.astype(jnp.bfloat16), grads[0].astype(jnp.bfloat16)))
    zeros = tuple((jnp.zeros(w.shape, jnp.float32) for w in weights))
    totals, (results, d_inputs) = lax.scan(step, zeros, (tokens, cotangent, positions))
    return (results, d_inputs, totals[0], totals[1], totals[2], totals[3], totals[4], totals[5], totals[6], totals[7], totals[8], totals[9], totals[10])
```

```python
import functools

import jax
import jax.numpy as jnp
import numpy as np
from jax import lax
from jax.experimental import pallas as pl
from jax.experimental.pallas import tpu as pltpu
from jax.sharding import PartitionSpec as P

HEADS = 16
KV_HEADS = 8
HEAD_DIM = 128
GROUP = HEADS // KV_HEADS
HALF = HEAD_DIM // 2
EPS = 1e-06
THETA = 1000000.0
AXES = ("dp", "ctx", "fsdp")
BF = jnp.bfloat16
F32 = jnp.float32


def dot(left, right, dims=((1,), (0,))):
    return lax.dot_general(left, right, (dims, ((), ())), preferred_element_type=F32)


NT = ((1,), (1,))
TN = ((0,), (0,))


def to_natural(nat_ref, src, dst, block, blocks):
    for b in range(blocks):
        row = pl.multiple_of(nat_ref[b] * block, block)
        dst[pl.ds(row, block), :] = src[b * block : (b + 1) * block, :]


def from_natural(nat_ref, src, dst, block, blocks):
    for b in range(blocks):
        row = pl.multiple_of(nat_ref[b] * block, block)
        dst[b * block : (b + 1) * block, :] = src[pl.ds(row, block), :].astype(dst.dtype)


def unit(lin):
    scale = lax.rsqrt(jnp.mean(lin * lin, axis=-1, keepdims=True) + EPS)
    return lin * scale, scale


def rope(values, cosine, sine):
    return values * cosine + pltpu.roll(values, HALF, 1) * sine


def unrope(values, cosine, sine):
    return values * cosine + pltpu.roll(values * sine, HALF, 1)


def stack_heads(values):
    return jnp.concatenate(
        [values[:, i * HEAD_DIM : (i + 1) * HEAD_DIM] for i in range(GROUP)], axis=0
    )


def unstack_heads(values, rows):
    return jnp.concatenate([values[i * rows : (i + 1) * rows] for i in range(GROUP)], axis=1)


def softmax_tile(query, key, tile, i):
    scores = lax.dot_general(query, key, (NT, ((), ())), preferred_element_type=F32)
    width = (i + 1) * tile
    row = lax.broadcasted_iota(jnp.int32, (GROUP * tile, width), 0) % tile + i * tile
    col = lax.broadcasted_iota(jnp.int32, (GROUP * tile, width), 1)
    scores = jnp.where(col <= row, scores, -1e30)
    highest = jnp.max(scores, axis=-1, keepdims=True)
    exponent = jnp.exp(scores - highest)
    total = jnp.sum(exponent, axis=-1, keepdims=True)
    return exponent * (1.0 / total)


def prepare(lin_ref, cos_ref, sin_ref, gq_ref, gk_ref, nat_ref, q_nat, k_nat, v_nat, block, blocks):
    for b in range(blocks):
        row = pl.multiple_of(nat_ref[b] * block, block)
        rows = slice(b * block, (b + 1) * block)
        cosine, sine = cos_ref[rows, :], sin_ref[rows, :]
        for i in range(GROUP):
            cols = slice(i * HEAD_DIM, (i + 1) * HEAD_DIM)
            normed, _ = unit(lin_ref[rows, cols])
            q_nat[pl.ds(row, block), cols] = (
                rope(normed * gq_ref[...], cosine, sine) * HEAD_DIM**-0.5
            ).astype(BF)
        cols = slice(GROUP * HEAD_DIM, (GROUP + 1) * HEAD_DIM)
        normed, _ = unit(lin_ref[rows, cols])
        k_nat[pl.ds(row, block), :] = rope(normed * gk_ref[...], cosine, sine).astype(BF)
        cols = slice((GROUP + 1) * HEAD_DIM, (GROUP + 2) * HEAD_DIM)
        v_nat[pl.ds(row, block), :] = lin_ref[rows, cols].astype(BF)


def attend_kernel(
    block, blocks, tile, nat_ref, lin_ref, cos_ref, sin_ref, gq_ref, gk_ref, o_ref, q_nat, k_nat, v_nat, o_nat
):
    prepare(lin_ref, cos_ref, sin_ref, gq_ref, gk_ref, nat_ref, q_nat, k_nat, v_nat, block, blocks)
    for i in range(blocks * block // tile):
        width = (i + 1) * tile
        rows = slice(i * tile, width)
        probs = softmax_tile(stack_heads(q_nat[rows, :]), k_nat[:width, :], tile, i).astype(BF)
        out = jnp.dot(probs, v_nat[:width, :], preferred_element_type=F32)
        o_nat[rows, :] = unstack_heads(out, tile).astype(BF)
    from_natural(nat_ref, o_nat, o_ref, block, blocks)


def attend_back_kernel(
    block, blocks, tile, nat_ref, lin_ref, do_ref, cos_ref, sin_ref, gq_ref, gk_ref,
    d_ref, dgq_ref, dgk_ref, q_nat, k_nat, v_nat, do_nat, dq_nat, dk_nat, dv_nat
):
    @pl.when((pl.program_id(0) == 0) & (pl.program_id(1) == 0))
    def _():
        dgq_ref[...] = jnp.zeros_like(dgq_ref)
        dgk_ref[...] = jnp.zeros_like(dgk_ref)

    prepare(lin_ref, cos_ref, sin_ref, gq_ref, gk_ref, nat_ref, q_nat, k_nat, v_nat, block, blocks)
    to_natural(nat_ref, do_ref, do_nat, block, blocks)
    tiles = blocks * block // tile
    for i in reversed(range(tiles)):
        width = (i + 1) * tile
        rows = slice(i * tile, width)
        query, key, value = stack_heads(q_nat[rows, :]), k_nat[:width, :], v_nat[:width, :]
        grad = stack_heads(do_nat[rows, :])
        probs = softmax_tile(query, key, tile, i)
        d_probs = lax.dot_general(grad, value, (NT, ((), ())), preferred_element_type=F32)
        inner = jnp.sum(d_probs * probs, axis=-1, keepdims=True)
        d_scores = (probs * (d_probs - inner)).astype(BF)
        d_query = jnp.dot(d_scores, key, preferred_element_type=F32)
        dq_nat[rows, :] = unstack_heads(d_query, tile)
        d_key = lax.dot_general(d_scores, query, (TN, ((), ())), preferred_element_type=F32)
        d_value = lax.dot_general(
            probs.astype(BF), grad, (TN, ((), ())), preferred_element_type=F32
        )
        if i == tiles - 1:
            dk_nat[...] = d_key
            dv_nat[...] = d_value
        else:
            dk_nat[:width, :] += d_key
            dv_nat[:width, :] += d_value
    for b in range(blocks):
        row = pl.multiple_of(nat_ref[b] * block, block)
        rows = slice(b * block, (b + 1) * block)
        cosine, sine = cos_ref[rows, :], sin_ref[rows, :]
        for i in range(GROUP + 1):
            cols = slice(i * HEAD_DIM, (i + 1) * HEAD_DIM)
            normed, scale = unit(lin_ref[rows, cols])
            if i < GROUP:
                grad = unrope(dq_nat[pl.ds(row, block), cols] * HEAD_DIM**-0.5, cosine, sine)
                gain_ref, total_ref = gq_ref, dgq_ref
            else:
                grad = unrope(dk_nat[pl.ds(row, block), :], cosine, sine)
                gain_ref, total_ref = gk_ref, dgk_ref
            total_ref[0:1, :] += jnp.sum(grad * normed, axis=0, keepdims=True)
            grad = grad * gain_ref[...]
            grad = scale * (grad - normed * jnp.mean(grad * normed, axis=-1, keepdims=True))
            d_ref[rows, cols] = grad.astype(BF)
        cols = slice((GROUP + 1) * HEAD_DIM, (GROUP + 2) * HEAD_DIM)
        d_ref[rows, cols] = dv_nat[pl.ds(row, block), :].astype(BF)


VMEM_LIMIT = 56 * 1024 * 1024


def attend(lin, cosine, sine, gq, gk, nat, seqs, heads, block):
    tokens = lin.shape[0]
    length = tokens // seqs
    blocks = length // block
    tile = min(256, length)
    width = (GROUP + 2) * HEAD_DIM
    table = pl.BlockSpec((length, HEAD_DIM), lambda s, h, n: (s, 0))
    gain = pl.BlockSpec((1, HEAD_DIM), lambda s, h, n: (0, 0))
    work = seqs * heads * GROUP * length * length * HEAD_DIM
    return pl.pallas_call(
        functools.partial(attend_kernel, block, blocks, tile),
        grid_spec=pltpu.PrefetchScalarGridSpec(
            num_scalar_prefetch=1,
            grid=(seqs, heads),
            in_specs=[pl.BlockSpec((length, width), lambda s, h, n: (s, h)), table, table, gain, gain],
            out_specs=pl.BlockSpec((length, GROUP * HEAD_DIM), lambda s, h, n: (s, h)),
            scratch_shapes=[
                pltpu.VMEM((length, GROUP * HEAD_DIM), BF),
                pltpu.VMEM((length, HEAD_DIM), BF),
                pltpu.VMEM((length, HEAD_DIM), BF),
                pltpu.VMEM((length, GROUP * HEAD_DIM), BF),
            ],
        ),
        out_shape=jax.ShapeDtypeStruct((tokens, heads * GROUP * HEAD_DIM), BF),
        compiler_params=pltpu.CompilerParams(vmem_limit_bytes=VMEM_LIMIT),
        cost_estimate=pl.CostEstimate(
            flops=3 * work, bytes_accessed=lin.size * 4, transcendentals=work // HEAD_DIM
        ),
        name="attend",
    )(nat, lin, cosine, sine, gq, gk)


def attend_back(lin, d_out, cosine, sine, gq, gk, nat, seqs, heads, block):
    tokens = lin.shape[0]
    length = tokens // seqs
    blocks = length // block
    tile = min(256, length)
    width = (GROUP + 2) * HEAD_DIM
    table = pl.BlockSpec((length, HEAD_DIM), lambda s, h, n: (s, 0))
    gain = pl.BlockSpec((1, HEAD_DIM), lambda s, h, n: (0, 0))
    total = pl.BlockSpec((8, HEAD_DIM), lambda s, h, n: (0, 0))
    work = seqs * heads * GROUP * length * length * HEAD_DIM
    return pl.pallas_call(
        functools.partial(attend_back_kernel, block, blocks, tile),
        grid_spec=pltpu.PrefetchScalarGridSpec(
            num_scalar_prefetch=1,
            grid=(seqs, heads),
            in_specs=[
                pl.BlockSpec((length, width), lambda s, h, n: (s, h)),
                pl.BlockSpec((length, GROUP * HEAD_DIM), lambda s, h, n: (s, h)),
                table, table, gain, gain,
            ],
            out_specs=[pl.BlockSpec((length, width), lambda s, h, n: (s, h)), total, total],
            scratch_shapes=[
                pltpu.VMEM((length, GROUP * HEAD_DIM), BF),
                pltpu.VMEM((length, HEAD_DIM), BF),
                pltpu.VMEM((length, HEAD_DIM), BF),
                pltpu.VMEM((length, GROUP * HEAD_DIM), BF),
                pltpu.VMEM((length, GROUP * HEAD_DIM), F32),
                pltpu.VMEM((length, HEAD_DIM), F32),
                pltpu.VMEM((length, HEAD_DIM), F32),
            ],
        ),
        out_shape=[
            jax.ShapeDtypeStruct((tokens, heads * width), BF),
            jax.ShapeDtypeStruct((8, HEAD_DIM), F32),
            jax.ShapeDtypeStruct((8, HEAD_DIM), F32),
        ],
        compiler_params=pltpu.CompilerParams(vmem_limit_bytes=VMEM_LIMIT),
        cost_estimate=pl.CostEstimate(
            flops=7 * work, bytes_accessed=lin.size * 8, transcendentals=work // HEAD_DIM
        ),
        name="attend_back",
    )(nat, lin, d_out, cosine, sine, gq, gk)


class Grid:
    def __init__(self, mesh):
        self.Z, self.Y, self.F = (mesh.shape[n] for n in AXES)
        self.C = 2 if self.F % 2 == 0 and KV_HEADS % (2 * self.Y) == 0 else 1
        self.A = self.F // self.C
        self.T = self.Y * self.C
        self.ZA = self.Z * self.A
        self.shape = (self.Z, self.Y, self.A, self.C)

    def index(self):
        f = lax.axis_index("fsdp")
        return lax.axis_index("dp"), lax.axis_index("ctx"), f // self.C, f % self.C

    def permute(self, value, target):
        pairs = []
        for i in range(int(np.prod(self.shape))):
            at = np.unravel_index(i, self.shape)
            pairs.append((i, int(np.ravel_multi_index(target(*(int(k) for k in at)), self.shape))))
        return lax.ppermute(value, AXES, pairs)

    def send(self, value, z=0, y=0, a=0, c=0):
        return self.permute(
            value,
            lambda i, j, k, l: ((i + z) % self.Z, (j + y) % self.Y, (k + a) % self.A, (l + c) % self.C),
        )


def on_device(
    grid, tokens, cotangent, positions, block_map, w_query, w_key, w_value, w_output, w_gate, w_up, w_down,
    gain_attn, gain_mlp, gain_query, gain_key,
):
    Z, Y, A, C, T, ZA = grid.Z, grid.Y, grid.A, grid.C, grid.T, grid.ZA
    send = grid.send
    z, y, a, c = grid.index()
    seq_count, local_rows, width = tokens.shape
    rows = seq_count * local_rows
    block = local_rows // 2
    group_tokens = T * rows
    seqs = C * seq_count
    hidden_units = w_gate.shape[1]
    heads = KV_HEADS // T

    def gather_tokens(own):
        chunks = [None] * Y
        chunks[0] = held = own
        for k in range(1, Y):
            held = send(held, y=1)
            chunks[Y - k] = held
        parts = list(chunks)
        if C == 2:
            parts += [send(chunk, c=1) for chunk in chunks]
        return jnp.concatenate(parts, axis=0)

    def scatter_tokens(partial):
        parts = partial.reshape(C, Y, rows, width)
        if C == 2:
            other = [send(parts[1, j], c=1) for j in range(Y)]
            summed = [parts[0, j].astype(F32) + other[j].astype(F32) for j in range(Y)]
        else:
            summed = [parts[0, j].astype(F32) for j in range(Y)]
        total = summed[Y - 1]
        for k in range(1, Y):
            total = send(total.astype(BF), y=1).astype(F32) + summed[Y - 1 - k]
        return total

    def gather_blocks(own):
        buffer = jnp.zeros((Z, A) + own.shape, own.dtype)
        held = own
        for s in range(Z):
            if s:
                held = send(held, z=1)
            piece = held
            for k in range(A):
                if k:
                    piece = send(piece, a=1)
                buffer = lax.dynamic_update_slice(
                    buffer, piece[None, None], ((z - s) % Z, (a - k) % A) + (0,) * own.ndim
                )
        return buffer

    def scatter_blocks(partial):
        def term(i, j):
            at = ((z + i) % Z, (a + j) % A) + (0,) * (partial.ndim - 2)
            return lax.dynamic_slice(partial, at, (1, 1) + partial.shape[2:])[0, 0].astype(F32)

        def over_a(i):
            total = term(i, A - 1)
            for k in range(1, A):
                total = send(total.astype(BF), a=1).astype(F32) + term(i, A - 1 - k)
            return total

        total = over_a(Z - 1)
        for s in range(1, Z):
            total = send(total.astype(BF), z=1).astype(F32) + over_a(Z - 1 - s)
        return total

    def own_columns(shard):
        own = lax.dynamic_slice_in_dim(shard, y * C + c, 1, 1)[:, 0]
        if C == 1:
            return own
        other = send(lax.dynamic_slice_in_dim(shard, y * C + (1 - c), 1, 1)[:, 0], c=1)
        return jnp.concatenate([jnp.where(c == 0, own, other), jnp.where(c == 0, other, own)], axis=0)

    def shard_of_columns(total):
        total = total.astype(BF)
        if C == 2:
            pair = total.reshape(2, -1, total.shape[-1])
            own = lax.dynamic_index_in_dim(pair, c, 0, keepdims=False)
            other = send(lax.dynamic_index_in_dim(pair, 1 - c, 0, keepdims=False), c=1)
            own = jnp.stack([jnp.where(c == 0, own, other), jnp.where(c == 0, other, own)], axis=1)
        else:
            own = total[:, None]
        whole = jnp.zeros((own.shape[0], Y) + own.shape[1:], F32)
        held = own
        for k in range(Y):
            if k:
                held = send(held, y=1)
            whole = lax.dynamic_update_slice(
                whole, held[:, None].astype(F32), (0, (y - k) % Y, 0, 0)
            )
        return whole

    shard_rows = w_query.shape[0]
    pack = jnp.concatenate([gain_attn, gain_mlp, gain_query, gain_key])
    qkv_width = (GROUP + 2) * HEAD_DIM * KV_HEADS // T
    pack = jnp.pad(pack, (0, qkv_width * 8 - pack.shape[0])).reshape(8, 1, qkv_width)
    qkv_shard = jnp.concatenate(
        [
            w_query.reshape(shard_rows, KV_HEADS, GROUP * HEAD_DIM),
            w_key.reshape(shard_rows, KV_HEADS, HEAD_DIM),
            w_value.reshape(shard_rows, KV_HEADS, HEAD_DIM),
        ],
        axis=2,
    ).reshape(shard_rows, T, qkv_width)
    qkv_shard = jnp.concatenate([qkv_shard, jnp.broadcast_to(pack, (8, T, qkv_width))], axis=0)

    x_group = gather_tokens(tokens.reshape(rows, width))
    place = gather_tokens(positions.reshape(rows, 1))[:, 0]

    qkv_all = gather_blocks(own_columns(qkv_shard)).reshape(ZA * C, shard_rows + 8, qkv_width)
    w_qkv = qkv_all[:, :shard_rows].reshape(width, qkv_width)
    packs = qkv_all[:, shard_rows:].reshape(ZA * C, -1)
    n, m = gain_attn.shape[0], gain_query.shape[0]
    ga = packs[:, :n].reshape(1, width).astype(F32)
    gm = packs[:, n : 2 * n].reshape(1, width).astype(F32)
    gq = packs[:, 2 * n : 2 * n + m].reshape(1, HEAD_DIM).astype(F32)
    gk = packs[:, 2 * n + m : 2 * n + 2 * m].reshape(1, HEAD_DIM).astype(F32)

    def out_target(i, j, k, l):
        b = ((i * A + k) * C + l) * Y + j
        rank, at = b // ZA, b % ZA
        return (at // A, rank // C, at % A, rank % C)

    def out_source(i, j, k, l):
        b = (j * C + l) * ZA + i * A + k
        shard, copy = b // Y, b % Y
        return (shard // C // A, copy, shard // C % A, shard % C)

    out_rows = w_output.shape[0] // Y
    wo_block = grid.permute(lax.dynamic_slice_in_dim(w_output, y * out_rows, out_rows, 0), out_target)
    w_out = gather_blocks(wo_block).reshape(-1, width)

    down_rows = w_down.shape[0] // Y

    def hidden_columns(shard):
        split = shard.reshape(shard.shape[0], ZA, C, Y, down_rows)
        return split.transpose(0, 3, 2, 1, 4).reshape(shard.shape[0], T, ZA * down_rows)

    w_g = gather_blocks(own_columns(hidden_columns(w_gate))).reshape(width, -1)
    w_u = gather_blocks(own_columns(hidden_columns(w_up))).reshape(width, -1)
    w_d = gather_blocks(lax.dynamic_slice_in_dim(w_down, y * down_rows, down_rows, 0)).reshape(-1, width)

    freqs = THETA ** (-(jnp.arange(HALF, dtype=F32) * 2.0 / HEAD_DIM))
    angles = place.astype(F32)[:, None] * freqs
    cosine, sine = jnp.cos(angles), jnp.sin(angles)
    cosine = jnp.concatenate([cosine, cosine], axis=1)
    sine = jnp.concatenate([-sine, sine], axis=1)
    order = (jnp.arange(Y, dtype=jnp.int32) + y) % Y
    nat = jnp.take(block_map.reshape(Y, 2), order, axis=0).reshape(-1)

    def unit_rows(values):
        scale = lax.rsqrt(jnp.mean(values * values, axis=-1, keepdims=True) + EPS)
        return values * scale, scale

    def norm_back(grad, gain, normed, scale):
        grad = grad * gain
        return scale * (grad - normed * jnp.mean(grad * normed, axis=-1, keepdims=True))

    x_unit, _ = unit_rows(x_group.astype(F32))
    h1 = (x_unit * ga).astype(BF)
    lin = dot(h1, w_qkv)
    attended = attend(lin, cosine, sine, gq, gk, nat, seqs, heads, block)
    x_own = tokens.reshape(rows, width).astype(F32)
    x_mid = x_own + scatter_tokens(dot(attended, w_out).astype(BF))

    mid_unit, mid_scale = unit_rows(x_mid)
    h2 = gather_tokens((mid_unit * gm).astype(BF))
    dy = gather_tokens(cotangent.reshape(rows, width))
    gate = dot(h2, w_g)
    upper = dot(h2, w_u)
    sigmoid = 1.0 / (1.0 + jnp.exp(-gate))
    silu = gate * sigmoid
    hidden = (silu * upper).astype(BF)
    gate_factor = (upper * sigmoid * (1.0 + gate * (1.0 - sigmoid))).astype(BF)
    upper_factor = silu.astype(BF)
    grad_down = dot(hidden, dy, TN).astype(BF)
    output = x_mid + scatter_tokens(dot(hidden, w_d).astype(BF))
    d_hidden = dot(dy, w_d, NT)
    d_gate = (d_hidden * gate_factor.astype(F32)).astype(BF)
    d_upper = (d_hidden * upper_factor.astype(F32)).astype(BF)
    d_h2 = scatter_tokens((dot(d_gate, w_g, NT) + dot(d_upper, w_u, NT)).astype(BF))
    grad_gate = dot(h2, d_gate, TN).astype(BF)
    grad_up = dot(h2, d_upper, TN).astype(BF)
    sum_mlp = jnp.sum(d_h2 * mid_unit, axis=0)
    d_mid = cotangent.reshape(rows, width).astype(F32) + norm_back(d_h2, gm, mid_unit, mid_scale)

    d_branch = gather_tokens(d_mid.astype(BF))
    d_attended = dot(d_branch, w_out, NT).astype(BF)
    grad_output = dot(attended, d_branch, TN).astype(BF)
    d_lin, sum_query, sum_key = attend_back(
        lin, d_attended, cosine, sine, gq, gk, nat, seqs, heads, block
    )
    grad_qkv = dot(h1, d_lin, TN).astype(BF)
    d_h1_part = dot(d_lin, w_qkv, NT)
    sum_attn = jnp.sum(d_h1_part * x_unit, axis=0)
    d_h1 = scatter_tokens(d_h1_part.astype(BF))
    own_unit, own_scale = unit_rows(x_own)
    grad_tokens = d_mid + norm_back(d_h1, ga, own_unit, own_scale)

    def columns_grad(partial):
        return shard_of_columns(scatter_blocks(partial.reshape(Z, A, -1, partial.shape[-1])))

    def hidden_grad(partial):
        whole = columns_grad(partial).reshape(shard_rows, Y, C, ZA, down_rows)
        return whole.transpose(0, 3, 2, 1, 4).reshape(shard_rows, hidden_units)

    def y_copies(own):
        whole = jnp.zeros((Y,) + own.shape, F32)
        held = own.astype(BF)
        for k in range(Y):
            if k:
                held = send(held, y=1)
            whole = lax.dynamic_update_slice(whole, held[None].astype(F32), ((y - k) % Y, 0, 0))
        return whole.reshape(-1, own.shape[-1])

    g_down = y_copies(scatter_blocks(grad_down.reshape(Z, A, down_rows, width)))
    g_gate = hidden_grad(grad_gate)
    g_up = hidden_grad(grad_up)
    g_out = scatter_blocks(grad_output.reshape(Z, A, -1, width)).astype(BF)
    g_out = y_copies(grid.permute(g_out, out_source))
    g_qkv = columns_grad(grad_qkv).reshape(shard_rows, KV_HEADS, (GROUP + 2) * HEAD_DIM)
    g_query = g_qkv[:, :, : GROUP * HEAD_DIM].reshape(shard_rows, -1)
    g_key = g_qkv[:, :, GROUP * HEAD_DIM : (GROUP + 1) * HEAD_DIM].reshape(shard_rows, -1)
    g_value = g_qkv[:, :, (GROUP + 1) * HEAD_DIM :].reshape(shard_rows, -1)

    sums = lax.psum(
        jnp.concatenate([sum_attn, sum_mlp, sum_query[0], sum_key[0]]), AXES
    )
    shard = (z * A + a) * C + c
    s_attn = lax.dynamic_slice_in_dim(sums, shard * n, n)
    s_mlp = lax.dynamic_slice_in_dim(sums, width + shard * n, n)
    s_query = lax.dynamic_slice_in_dim(sums, 2 * width + shard * m, m)
    s_key = lax.dynamic_slice_in_dim(sums, 2 * width + HEAD_DIM + shard * m, m)
    return (
        output.astype(BF).reshape(tokens.shape), grad_tokens.astype(BF).reshape(tokens.shape),
        g_query, g_key, g_value, g_out, g_gate, g_up, g_down, s_attn, s_mlp, s_query, s_key,
    )


def solution(mesh):
    sharded = P(("dp", "fsdp"), None)
    vector = P(("dp", "fsdp"))
    tokens = P(("dp", "fsdp"), "ctx", None)
    return jax.shard_map(
        functools.partial(on_device, Grid(mesh)),
        mesh=mesh,
        in_specs=(tokens, tokens, P(("dp", "fsdp"), "ctx"), P()) + (sharded,) * 7 + (vector,) * 4,
        out_specs=(tokens, tokens) + (sharded,) * 7 + (vector,) * 4,
        check_vma=False,
    )
```

```python
import functools

import jax
import jax.numpy as jnp
import numpy as np
from jax import lax
from jax.experimental import pallas as pl
from jax.experimental.pallas import tpu as pltpu
from jax.sharding import PartitionSpec as P

HEADS = 16
KV_HEADS = 8
HEAD_DIM = 128
GROUP = HEADS // KV_HEADS
HALF = HEAD_DIM // 2
EPS = 1e-06
THETA = 1000000.0
AXES = ("dp", "ctx", "fsdp")
BF = jnp.bfloat16
F32 = jnp.float32


def dot(left, right, dims=((1,), (0,))):
    return lax.dot_general(left, right, (dims, ((), ())), preferred_element_type=F32)


NT = ((1,), (1,))
TN = ((0,), (0,))


def to_natural(nat_ref, src, dst, block, blocks):
    for b in range(blocks):
        row = pl.multiple_of(nat_ref[b] * block, block)
        dst[pl.ds(row, block), :] = src[b * block : (b + 1) * block, :]


def from_natural(nat_ref, src, dst, block, blocks):
    for b in range(blocks):
        row = pl.multiple_of(nat_ref[b] * block, block)
        dst[b * block : (b + 1) * block, :] = src[pl.ds(row, block), :].astype(dst.dtype)


def unit(lin):
    scale = lax.rsqrt(jnp.mean(lin * lin, axis=-1, keepdims=True) + EPS)
    return lin * scale, scale


def rope(values, cosine, sine):
    return values * cosine + pltpu.roll(values, HALF, 1) * sine


def unrope(values, cosine, sine):
    return values * cosine + pltpu.roll(values * sine, HALF, 1)


def stack_heads(values):
    return jnp.concatenate(
        [values[:, i * HEAD_DIM : (i + 1) * HEAD_DIM] for i in range(GROUP)], axis=0
    )


def unstack_heads(values, rows):
    return jnp.concatenate([values[i * rows : (i + 1) * rows] for i in range(GROUP)], axis=1)


def softmax_tile(query, key, tile, i):
    scores = lax.dot_general(query, key, (NT, ((), ())), preferred_element_type=F32)
    width = (i + 1) * tile
    row = lax.broadcasted_iota(jnp.int32, (GROUP * tile, width), 0) % tile + i * tile
    col = lax.broadcasted_iota(jnp.int32, (GROUP * tile, width), 1)
    scores = jnp.where(col <= row, scores, -1e30)
    highest = jnp.max(scores, axis=-1, keepdims=True)
    exponent = jnp.exp(scores - highest)
    total = jnp.sum(exponent, axis=-1, keepdims=True)
    return exponent * (1.0 / total)


def prepare(lin_ref, cos_ref, sin_ref, gq_ref, gk_ref, nat_ref, q_nat, k_nat, v_nat, block, blocks):
    for b in range(blocks):
        row = pl.multiple_of(nat_ref[b] * block, block)
        rows = slice(b * block, (b + 1) * block)
        cosine, sine = cos_ref[rows, :], sin_ref[rows, :]
        for i in range(GROUP):
            cols = slice(i * HEAD_DIM, (i + 1) * HEAD_DIM)
            normed, _ = unit(lin_ref[rows, cols])
            q_nat[pl.ds(row, block), cols] = (
                rope(normed * gq_ref[...], cosine, sine) * HEAD_DIM**-0.5
            ).astype(BF)
        cols = slice(GROUP * HEAD_DIM, (GROUP + 1) * HEAD_DIM)
        normed, _ = unit(lin_ref[rows, cols])
        k_nat[pl.ds(row, block), :] = rope(normed * gk_ref[...], cosine, sine).astype(BF)
        cols = slice((GROUP + 1) * HEAD_DIM, (GROUP + 2) * HEAD_DIM)
        v_nat[pl.ds(row, block), :] = lin_ref[rows, cols].astype(BF)


def attend_kernel(
    block, blocks, tile, nat_ref, lin_ref, cos_ref, sin_ref, gq_ref, gk_ref, o_ref, q_nat, k_nat, v_nat, o_nat
):
    prepare(lin_ref, cos_ref, sin_ref, gq_ref, gk_ref, nat_ref, q_nat, k_nat, v_nat, block, blocks)
    for i in range(blocks * block // tile):
        width = (i + 1) * tile
        rows = slice(i * tile, width)
        probs = softmax_tile(stack_heads(q_nat[rows, :]), k_nat[:width, :], tile, i).astype(BF)
        out = jnp.dot(probs, v_nat[:width, :], preferred_element_type=F32)
        o_nat[rows, :] = unstack_heads(out, tile).astype(BF)
    from_natural(nat_ref, o_nat, o_ref, block, blocks)


def attend_back_kernel(
    block, blocks, tile, nat_ref, lin_ref, do_ref, cos_ref, sin_ref, gq_ref, gk_ref,
    d_ref, dgq_ref, dgk_ref, q_nat, k_nat, v_nat, do_nat, dq_nat, dk_nat, dv_nat
):
    @pl.when((pl.program_id(0) == 0) & (pl.program_id(1) == 0))
    def _():
        dgq_ref[...] = jnp.zeros_like(dgq_ref)
        dgk_ref[...] = jnp.zeros_like(dgk_ref)

    prepare(lin_ref, cos_ref, sin_ref, gq_ref, gk_ref, nat_ref, q_nat, k_nat, v_nat, block, blocks)
    to_natural(nat_ref, do_ref, do_nat, block, blocks)
    tiles = blocks * block // tile
    for i in reversed(range(tiles)):
        width = (i + 1) * tile
        rows = slice(i * tile, width)
        query, key, value = stack_heads(q_nat[rows, :]), k_nat[:width, :], v_nat[:width, :]
        grad = stack_heads(do_nat[rows, :])
        probs = softmax_tile(query, key, tile, i)
        d_probs = lax.dot_general(grad, value, (NT, ((), ())), preferred_element_type=F32)
        inner = jnp.sum(d_probs * probs, axis=-1, keepdims=True)
        d_scores = (probs * (d_probs - inner)).astype(BF)
        d_query = jnp.dot(d_scores, key, preferred_element_type=F32)
        dq_nat[rows, :] = unstack_heads(d_query, tile)
        d_key = lax.dot_general(d_scores, query, (TN, ((), ())), preferred_element_type=F32)
        d_value = lax.dot_general(
            probs.astype(BF), grad, (TN, ((), ())), preferred_element_type=F32
        )
        if i == tiles - 1:
            dk_nat[...] = d_key
            dv_nat[...] = d_value
        else:
            dk_nat[:width, :] += d_key
            dv_nat[:width, :] += d_value
    for b in range(blocks):
        row = pl.multiple_of(nat_ref[b] * block, block)
        rows = slice(b * block, (b + 1) * block)
        cosine, sine = cos_ref[rows, :], sin_ref[rows, :]
        for i in range(GROUP + 1):
            cols = slice(i * HEAD_DIM, (i + 1) * HEAD_DIM)
            normed, scale = unit(lin_ref[rows, cols])
            if i < GROUP:
                grad = unrope(dq_nat[pl.ds(row, block), cols] * HEAD_DIM**-0.5, cosine, sine)
                gain_ref, total_ref = gq_ref, dgq_ref
            else:
                grad = unrope(dk_nat[pl.ds(row, block), :], cosine, sine)
                gain_ref, total_ref = gk_ref, dgk_ref
            total_ref[0:1, :] += jnp.sum(grad * normed, axis=0, keepdims=True)
            grad = grad * gain_ref[...]
            grad = scale * (grad - normed * jnp.mean(grad * normed, axis=-1, keepdims=True))
            d_ref[rows, cols] = grad.astype(BF)
        cols = slice((GROUP + 1) * HEAD_DIM, (GROUP + 2) * HEAD_DIM)
        d_ref[rows, cols] = dv_nat[pl.ds(row, block), :].astype(BF)


VMEM_LIMIT = 56 * 1024 * 1024


def attend(lin, cosine, sine, gq, gk, nat, seqs, heads, block):
    tokens = lin.shape[0]
    length = tokens // seqs
    blocks = length // block
    tile = min(256, length)
    width = (GROUP + 2) * HEAD_DIM
    table = pl.BlockSpec((length, HEAD_DIM), lambda s, h, n: (s, 0))
    gain = pl.BlockSpec((1, HEAD_DIM), lambda s, h, n: (0, 0))
    work = seqs * heads * GROUP * length * length * HEAD_DIM
    return pl.pallas_call(
        functools.partial(attend_kernel, block, blocks, tile),
        grid_spec=pltpu.PrefetchScalarGridSpec(
            num_scalar_prefetch=1,
            grid=(seqs, heads),
            in_specs=[pl.BlockSpec((length, width), lambda s, h, n: (s, h)), table, table, gain, gain],
            out_specs=pl.BlockSpec((length, GROUP * HEAD_DIM), lambda s, h, n: (s, h)),
            scratch_shapes=[
                pltpu.VMEM((length, GROUP * HEAD_DIM), BF),
                pltpu.VMEM((length, HEAD_DIM), BF),
                pltpu.VMEM((length, HEAD_DIM), BF),
                pltpu.VMEM((length, GROUP * HEAD_DIM), BF),
            ],
        ),
        out_shape=jax.ShapeDtypeStruct((tokens, heads * GROUP * HEAD_DIM), BF),
        compiler_params=pltpu.CompilerParams(vmem_limit_bytes=VMEM_LIMIT),
        cost_estimate=pl.CostEstimate(
            flops=3 * work, bytes_accessed=lin.size * 4, transcendentals=work // HEAD_DIM
        ),
        name="attend",
    )(nat, lin, cosine, sine, gq, gk)


def attend_back(lin, d_out, cosine, sine, gq, gk, nat, seqs, heads, block):
    tokens = lin.shape[0]
    length = tokens // seqs
    blocks = length // block
    tile = min(256, length)
    width = (GROUP + 2) * HEAD_DIM
    table = pl.BlockSpec((length, HEAD_DIM), lambda s, h, n: (s, 0))
    gain = pl.BlockSpec((1, HEAD_DIM), lambda s, h, n: (0, 0))
    total = pl.BlockSpec((8, HEAD_DIM), lambda s, h, n: (0, 0))
    work = seqs * heads * GROUP * length * length * HEAD_DIM
    return pl.pallas_call(
        functools.partial(attend_back_kernel, block, blocks, tile),
        grid_spec=pltpu.PrefetchScalarGridSpec(
            num_scalar_prefetch=1,
            grid=(seqs, heads),
            in_specs=[
                pl.BlockSpec((length, width), lambda s, h, n: (s, h)),
                pl.BlockSpec((length, GROUP * HEAD_DIM), lambda s, h, n: (s, h)),
                table, table, gain, gain,
            ],
            out_specs=[pl.BlockSpec((length, width), lambda s, h, n: (s, h)), total, total],
            scratch_shapes=[
                pltpu.VMEM((length, GROUP * HEAD_DIM), BF),
                pltpu.VMEM((length, HEAD_DIM), BF),
                pltpu.VMEM((length, HEAD_DIM), BF),
                pltpu.VMEM((length, GROUP * HEAD_DIM), BF),
                pltpu.VMEM((length, GROUP * HEAD_DIM), F32),
                pltpu.VMEM((length, HEAD_DIM), F32),
                pltpu.VMEM((length, HEAD_DIM), F32),
            ],
        ),
        out_shape=[
            jax.ShapeDtypeStruct((tokens, heads * width), BF),
            jax.ShapeDtypeStruct((8, HEAD_DIM), F32),
            jax.ShapeDtypeStruct((8, HEAD_DIM), F32),
        ],
        compiler_params=pltpu.CompilerParams(vmem_limit_bytes=VMEM_LIMIT),
        cost_estimate=pl.CostEstimate(
            flops=7 * work, bytes_accessed=lin.size * 8, transcendentals=work // HEAD_DIM
        ),
        name="attend_back",
    )(nat, lin, d_out, cosine, sine, gq, gk)


ANY = pl.BlockSpec(memory_space=pl.ANY)
IN_VMEM = pl.BlockSpec(memory_space=pltpu.VMEM)
SEMAPHORES = 128


class Flight:
    def __init__(self, made, remote):
        self.made, self.remote, self.started, self.left = made, remote, False, True

    def start(self):
        self.made.start()

    def wait(self):
        if self.left:
            self.left = False
            if self.remote:
                self.made.wait_recv()
            else:
                self.made.wait()

    wait_recv = wait


class Mover:
    def __init__(self, grid, local_sems, send_sems, recv_sems):
        self.grid = grid
        self.z, self.y, self.a, self.c = grid.index()
        self.local_sems, self.send_sems, self.recv_sems = local_sems, send_sems, recv_sems
        self.locals, self.remotes, self.made_count = [], [], 0

    def device(self, z, y, a, c):
        return {"dp": z, "ctx": y, "fsdp": a * self.grid.C + c}

    def peer(self, z=0, y=0, a=0, c=0):
        g = self.grid
        return self.device(
            lax.rem(self.z + z + g.Z, g.Z), lax.rem(self.y + y + g.Y, g.Y),
            lax.rem(self.a + a + g.A, g.A), lax.rem(self.c + c + g.C, g.C),
        )

    def meet(self, extra=()):
        g = self.grid
        offsets = set()
        for axis, size in enumerate(g.shape):
            for step in (1, size - 1):
                if 0 < step < size:
                    offsets.add(tuple(step if i == axis else 0 for i in range(4)))
        barrier = pltpu.get_barrier_semaphore()
        for offset in sorted(offsets):
            pl.semaphore_signal(
                barrier, inc=1, device_id=self.peer(*offset), device_id_type=pl.DeviceIdType.MESH
            )
        for device, present in extra:

            @pl.when(present)
            def _(device=device):
                pl.semaphore_signal(
                    barrier, inc=1, device_id=device, device_id_type=pl.DeviceIdType.MESH
                )

        count = len(offsets)
        for _, present in extra:
            count = count + present.astype(jnp.int32)
        pl.semaphore_wait(barrier, count)

    def copy(self, src, dst):
        made = Flight(pltpu.make_async_copy(src, dst, self.local_sems.at[len(self.locals)]), False)
        self.locals.append(made)
        made.start()
        return made

    def make(self, src, dst, device):
        i = self.made_count
        made = pltpu.make_async_remote_copy(
            src_ref=src, dst_ref=dst, send_sem=self.send_sems.at[i], recv_sem=self.recv_sems.at[i],
            device_id=device, device_id_type=pl.DeviceIdType.MESH,
        )
        self.made_count = i + 1
        return made

    def send(self, src, dst, **to):
        made = Flight(self.make(src, dst, self.peer(**to)), True)
        self.remotes.append(made)
        made.start()
        return made

    def settle(self):
        for made in self.remotes:
            made.wait()
        for made in self.locals:
            made.wait()
        for made in self.remotes:
            made.made.wait_send()


def semaphores():
    return [pltpu.SemaphoreType.DMA((SEMAPHORES,)) for _ in range(3)]


class Ring:
    def __init__(self, mover, full):
        self.m, self.full = mover, full
        self.hops, self.sides = {}, {}

    def block(self, s, k=0):
        g = self.m.grid
        return self.full.at[
            lax.rem(self.m.z - s + g.Z, g.Z), lax.rem(self.m.a - k + g.A, g.A)
        ]

    def hop(self, s):
        src = self.block(s - 1)
        self.hops[s] = self.m.send(src, src, z=1)

    def landed(self, s):
        self.hops[s].wait_recv()

    def side(self, s):
        src = self.block(s)
        self.sides[s] = [self.m.send(src, src, a=1)]

    def finish_side(self, s):
        for k in range(1, self.m.grid.A):
            self.sides[s][k - 1].wait_recv()
            if k < self.m.grid.A - 1:
                src = self.block(s, k)
                self.sides[s].append(self.m.send(src, src, a=1))


def gather_start_kernel(
    grid, out_target, out_source, tok, pos, pack, qkv_pair, out_own, gate_pair, up_pair, down_own,
    tok_all, pos_all, qkv_full, out_full, gate_full, up_full, down_full,
    local_sems, send_sems, recv_sems,
):
    m = Mover(grid, local_sems, send_sems, recv_sems)
    Z, Y, A, C = grid.shape
    target, source = out_target(m.z, m.y, m.a, m.c), out_source(m.z, m.y, m.a, m.c)
    away = (target[0] != m.z) | (target[1] != m.y) | (target[2] != m.a) | (target[3] != m.c)
    m.meet([(m.device(*target), away), (m.device(*source), away)])

    class Tokens:
        def __init__(self, own, whole):
            self.own, self.whole, self.flights, self.cores = own, whole, {}, []

        def step(self, k):
            src = self.own if k == 1 else self.whole.at[0, Y - k + 1]
            self.flights[k] = m.send(src, self.whole.at[0, Y - k], y=1)

        def keep(self):
            if C == 2:
                m.send(self.own, self.whole.at[1, 0], c=1)
            m.copy(self.own, self.whole.at[0, 0])

        def landed(self, k):
            self.flights[k].wait_recv()
            if k < Y - 1:
                self.step(k + 1)
            if C == 2:
                m.send(self.whole.at[0, Y - k], self.whole.at[1, Y - k], c=1)

    toks, poss = Tokens(tok, tok_all), Tokens(pos, pos_all)

    class Pair:
        def __init__(self, own, other, mine, yours):
            self.local = m.copy(own, mine)
            self.other = m.send(other, yours, c=1) if C == 2 else None

        def wait(self):
            self.local.wait()
            if C == 2:
                self.other.wait_recv()

    def columns(shard, full):
        at = full.at[m.z, m.a, m.c]
        return Pair(shard.at[m.c], shard.at[(C - 1) * (1 - m.c)], at, at)

    rows = out_own.shape[0] // Y
    mine = out_own.at[pl.ds(pl.multiple_of(m.y * rows, rows), rows)]
    moved = m.make(mine, out_full.at[target[0], target[2], pl.ds(0, rows)], m.device(*target))
    stay = pltpu.make_async_copy(
        mine, out_full.at[m.z, m.a, pl.ds(0, rows)], m.local_sems.at[SEMAPHORES - 1]
    )

    @pl.when(away)
    def _():
        moved.start()

    @pl.when(jnp.logical_not(away))
    def _():
        stay.start()

    qkv_pairs = columns(qkv_pair, qkv_full)
    if Y > 1:
        poss.step(1)
        toks.step(1)
    at = out_full.at[m.z, m.a, pl.ds(pl.multiple_of(rows + m.c * 8, 8), 8)]
    packs = Pair(pack, pack, at, at)
    gate_pairs = columns(gate_pair, gate_full)
    qkv, out, gate = Ring(m, qkv_full), Ring(m, out_full), Ring(m, gate_full)
    qkv_pairs.wait()
    if Z > 1:
        qkv.hop(1)
    qkv.side(0)
    up_pairs = columns(up_pair, up_full)
    rows = down_own.shape[0] // Y
    m.copy(down_own.at[pl.ds(pl.multiple_of(m.y * rows, rows), rows)], down_full.at[m.z, m.a])
    for part in (toks, poss):
        part.keep()
    for k in range(1, Y):
        poss.landed(k)
    for s in range(1, Z):
        if s == Z - 1:
            for k in range(1, Y):
                toks.landed(k)
        qkv.landed(s)
        if s < Z - 1:
            qkv.hop(s + 1)
        qkv.side(s)
        if s == Z - 2:
            gate_pairs.wait()
            gate.hop(1)
    packs.wait()

    @pl.when(away)
    def _():
        moved.wait_recv()

    @pl.when(jnp.logical_not(away))
    def _():
        stay.wait()

    if Z > 1:
        out.hop(1)
    out.side(0)
    gate.side(0)
    if Z > 2:
        gate.landed(1)
        gate.hop(2)
    for s in range(1, Z):
        out.landed(s)
        if s < Z - 1:
            out.hop(s + 1)
        out.side(s)
    for ring in (qkv, out):
        for s in range(Z):
            ring.finish_side(s)
    gate.finish_side(0)
    m.settle()

    @pl.when(away)
    def _():
        moved.wait_send()


def weights_program(gate, up, down, Z):
    def first():
        if Z > 3:
            gate.hop(3)
        up.hop(1)
        for s in range(1, min(Z, 3)):
            gate.side(s)

    yield first
    for s in range(3, Z):

        def more(s=s):
            gate.landed(s)
            if s < Z - 1:
                gate.hop(s + 1)
            gate.side(s)

        yield more
    for s in range(1, Z):

        def rest(s=s):
            up.landed(s)
            if s < Z - 1:
                up.hop(s + 1)
            else:
                down.hop(1)
            if s == 1:
                up.side(0)
            up.side(s)

        yield rest
    for s in range(1, Z):

        def tail(s=s):
            down.landed(s)
            if s < Z - 1:
                down.hop(s + 1)

        yield tail

    def finish():
        for s in range(1, Z):
            gate.finish_side(s)
        for s in range(Z):
            up.finish_side(s)

    yield finish


def join_kernel(
    grid, halves, background, part, own, gain, gate_in, up_in, down_in,
    mid, h2, gate_full, up_full, down_full,
    mine, other, passing, landing, base, total, low, local_sems, send_sems, recv_sems,
):
    m = Mover(grid, local_sems, send_sems, recv_sems)
    Z, Y, A, C = grid.shape
    m.meet()
    rows = own.shape[0]
    n = rows // halves
    loads = {}
    crossings = {}
    for h in range(halves):
        for j in reversed(range(Y)):
            at = pl.ds(h * n, n)
            if C == 2:
                crossings[h, j] = m.send(part.at[1, j, at], other.at[j, at], c=1)
            loads[h, j] = m.copy(part.at[0, j, at], mine.at[j, at])
    own_load = m.copy(own, base)
    gate, up, down = Ring(m, gate_full), Ring(m, up_full), Ring(m, down_full)
    program = list(background(gate, up, down, Z))

    def run(count):
        for _ in range(min(count, len(program))):
            program.pop(0)()

    chunk = min(32, n)

    def each(h, body):
        @pl.loop(0, n // chunk)
        def _(i):
            body(pl.ds(pl.multiple_of(h * n + i * chunk, chunk), chunk))

    def summed(j, at):
        value = mine[j, at].astype(F32)
        return value + other[j, at].astype(F32) if C == 2 else value

    def ready(h, j):
        loads[h, j].wait()
        if C == 2:
            crossings[h, j].wait_recv()

    run(1)
    flights = {}
    for h in range(halves):
        ready(h, Y - 1)

        def first(at):
            passing[0, at] = summed(Y - 1, at).astype(BF)

        each(h, first)
        if Y > 1:
            at = pl.ds(h * n, n)
            flights[h, 1] = m.send(passing.at[0, at], landing.at[0, at], y=1)
    for k in range(2, Y):
        for h in range(halves):
            flights[h, k - 1].wait_recv()
            ready(h, Y - k)

            def middle(at, k=k):
                value = landing[k - 2, at].astype(F32) + summed(Y - k, at)
                passing[k - 1, at] = value.astype(BF)

            each(h, middle)
            at = pl.ds(h * n, n)
            flights[h, k] = m.send(passing.at[k - 1, at], landing.at[k - 1, at], y=1)
    own_load.wait()
    run(2)
    stores, spread = [], {}
    for h in range(halves):
        if Y > 1:
            ready(h, 0)
            flights[h, Y - 1].wait_recv()

        def last(at):
            value = base[at].astype(F32) + (
                summed(0, at) + landing[Y - 2, at].astype(F32) if Y > 1 else passing[0, at].astype(F32)
            )
            total[at] = value
            scale = lax.rsqrt(jnp.mean(value * value, axis=-1, keepdims=True) + EPS)
            low[at] = (value * scale * gain[...]).astype(BF)

        each(h, last)
        at = pl.ds(h * n, n)
        if Y > 1:
            spread[h, 1] = m.send(low.at[at], h2.at[0, Y - 1, at], y=1)
        if C == 2:
            spread[h, "core"] = m.send(low.at[at], h2.at[1, 0, at], c=1)
        stores.append(m.copy(low.at[at], h2.at[0, 0, at]))
        stores.append(m.copy(total.at[at], mid.at[at]))
        run(1)
    run(2)
    for k in range(1, Y):
        for h in range(halves):
            at = pl.ds(h * n, n)
            spread[h, k].wait_recv()
            if k < Y - 1:
                spread[h, k + 1] = m.send(h2.at[0, Y - k, at], h2.at[0, Y - k - 1, at], y=1)
            if C == 2:
                spread[h, "core", k] = m.send(h2.at[0, Y - k, at], h2.at[1, Y - k, at], c=1)
    run(len(program))
    m.settle()


def gather_start(grid, targets, tok, pos, pack, qkv_pair, out_own, gate_pair, up_pair, down_own):
    Z, Y, A, C = grid.shape

    def whole(own, *lead):
        return jax.ShapeDtypeStruct(lead + own.shape, own.dtype)

    def cut(own):
        return jax.ShapeDtypeStruct((Z, A, own.shape[0] // Y) + own.shape[1:], own.dtype)

    shapes = [whole(tok, C, Y), whole(pos, C, Y), whole(qkv_pair, Z, A)]
    out_rows = out_own.shape[0] // Y + 8 * C
    shapes += [jax.ShapeDtypeStruct((Z, A, out_rows, out_own.shape[1]), BF), whole(gate_pair, Z, A), whole(up_pair, Z, A), cut(down_own)]
    return pl.pallas_call(
        functools.partial(gather_start_kernel, grid, *targets),
        out_shape=shapes,
        in_specs=[IN_VMEM] * 8,
        out_specs=[ANY] * 7,
        scratch_shapes=semaphores(),
        compiler_params=pltpu.CompilerParams(
            collective_id=0, has_side_effects=True, vmem_limit_bytes=32 * 1024 * 1024
        ),
        cost_estimate=pl.CostEstimate(flops=0, bytes_accessed=300_000_000, transcendentals=0),
        name="gather_start",
    )(tok, pos, pack, qkv_pair, out_own, gate_pair, up_pair, down_own)


def join(grid, part, own, gain, gate, up, down):
    Z, Y, A, C = grid.shape
    rows, width = own.shape
    halves = 2 if rows % 64 == 0 else 1
    hops = max(Y - 1, 1)
    return pl.pallas_call(
        functools.partial(join_kernel, grid, halves, weights_program),
        out_shape=[
            jax.ShapeDtypeStruct((rows, width), F32),
            jax.ShapeDtypeStruct((C, Y, rows, width), BF),
            jax.ShapeDtypeStruct(gate.shape, gate.dtype),
            jax.ShapeDtypeStruct(up.shape, up.dtype),
            jax.ShapeDtypeStruct(down.shape, down.dtype),
        ],
        in_specs=[ANY, ANY, IN_VMEM, ANY, ANY, ANY],
        out_specs=[ANY] * 5,
        input_output_aliases={3: 2, 4: 3, 5: 4},
        scratch_shapes=[
            pltpu.VMEM((Y, rows, width), BF),
            pltpu.VMEM((Y, rows, width), BF),
            pltpu.VMEM((hops, rows, width), BF),
            pltpu.VMEM((hops, rows, width), BF),
            pltpu.VMEM((rows, width), BF),
            pltpu.VMEM((rows, width), F32),
            pltpu.VMEM((rows, width), BF),
            *semaphores(),
        ],
        compiler_params=pltpu.CompilerParams(
            collective_id=1, has_side_effects=True, vmem_limit_bytes=40 * 1024 * 1024
        ),
        cost_estimate=pl.CostEstimate(flops=0, bytes_accessed=300_000_000, transcendentals=0),
        name="join",
    )(part.reshape(C, Y, rows, width), own, gain, gate, up, down)


def after(tokens, *values):
    out = lax.optimization_barrier((*values, *tokens))
    return out[0] if len(values) == 1 else out[: len(values)]


class Grid:
    def __init__(self, mesh):
        self.Z, self.Y, self.F = (mesh.shape[n] for n in AXES)
        self.C = 2 if self.F % 2 == 0 and KV_HEADS % (2 * self.Y) == 0 else 1
        self.A = self.F // self.C
        self.T = self.Y * self.C
        self.ZA = self.Z * self.A
        self.shape = (self.Z, self.Y, self.A, self.C)

    def index(self):
        f = lax.axis_index("fsdp")
        return lax.axis_index("dp"), lax.axis_index("ctx"), f // self.C, f % self.C

    def permute(self, value, target):
        pairs = []
        for i in range(int(np.prod(self.shape))):
            at = np.unravel_index(i, self.shape)
            pairs.append((i, int(np.ravel_multi_index(target(*(int(k) for k in at)), self.shape))))
        return lax.ppermute(value, AXES, pairs)

    def send(self, value, z=0, y=0, a=0, c=0):
        return self.permute(
            value,
            lambda i, j, k, l: ((i + z) % self.Z, (j + y) % self.Y, (k + a) % self.A, (l + c) % self.C),
        )


def on_device(
    grid, tokens, cotangent, positions, block_map, w_query, w_key, w_value, w_output, w_gate, w_up, w_down,
    gain_attn, gain_mlp, gain_query, gain_key,
):
    Z, Y, A, C, T, ZA = grid.Z, grid.Y, grid.A, grid.C, grid.T, grid.ZA
    send = grid.send
    z, y, a, c = grid.index()
    seq_count, local_rows, width = tokens.shape
    rows = seq_count * local_rows
    block = local_rows // 2
    group_tokens = T * rows
    seqs = C * seq_count
    hidden_units = w_gate.shape[1]
    heads = KV_HEADS // T

    def gather_tokens(own):
        chunks = [None] * Y
        chunks[0] = held = own
        for k in range(1, Y):
            held = send(held, y=1)
            chunks[Y - k] = held
        parts = list(chunks)
        if C == 2:
            parts += [send(chunk, c=1) for chunk in chunks]
        return jnp.concatenate(parts, axis=0)

    def scatter_tokens(partial):
        parts = partial.reshape(C, Y, rows, width)
        if C == 2:
            other = [send(parts[1, j], c=1) for j in range(Y)]
            summed = [parts[0, j].astype(F32) + other[j].astype(F32) for j in range(Y)]
        else:
            summed = [parts[0, j].astype(F32) for j in range(Y)]
        total = summed[Y - 1]
        for k in range(1, Y):
            total = send(total.astype(BF), y=1).astype(F32) + summed[Y - 1 - k]
        return total

    def shard_of_columns(total):
        total = total.astype(BF)
        if C == 2:
            pair = total.reshape(2, -1, total.shape[-1])
            own = lax.dynamic_index_in_dim(pair, c, 0, keepdims=False)
            other = send(lax.dynamic_index_in_dim(pair, 1 - c, 0, keepdims=False), c=1)
            own = jnp.stack([jnp.where(c == 0, own, other), jnp.where(c == 0, other, own)], axis=1)
        else:
            own = total[:, None]
        whole = jnp.zeros((own.shape[0], Y) + own.shape[1:], F32)
        held = own
        for k in range(Y):
            if k:
                held = send(held, y=1)
            whole = lax.dynamic_update_slice(
                whole, held[:, None].astype(F32), (0, (y - k) % Y, 0, 0)
            )
        return whole

    shard_rows = w_query.shape[0]
    n, m = gain_attn.shape[0], gain_query.shape[0]
    pack = jnp.concatenate([gain_attn, gain_mlp, gain_query, gain_key])
    pack = jnp.pad(pack, (0, 8 * width - pack.shape[0])).reshape(8, width)
    qkv_width = (GROUP + 2) * HEAD_DIM * KV_HEADS // T
    qkv_shard = jnp.concatenate(
        [
            w_query.reshape(shard_rows, KV_HEADS, GROUP * HEAD_DIM),
            w_key.reshape(shard_rows, KV_HEADS, HEAD_DIM),
            w_value.reshape(shard_rows, KV_HEADS, HEAD_DIM),
        ],
        axis=2,
    ).reshape(shard_rows, T, qkv_width)

    def out_target(i, j, k, l):
        b = ((i * A + k) * C + l) * Y + j
        rank, at = b // ZA, b % ZA
        return (at // A, rank // C, at % A, rank % C)

    def out_source(i, j, k, l):
        b = (j * C + l) * ZA + i * A + k
        shard, copy = b // Y, b % Y
        return (shard // C // A, copy, shard // C % A, shard % C)

    down_rows = w_down.shape[0] // Y

    def hidden_columns(shard):
        split = shard.reshape(shard.shape[0], ZA, C, Y, down_rows)
        return split.transpose(0, 3, 2, 1, 4).reshape(shard.shape[0], T, ZA * down_rows)

    def own_pair(shard):
        return lax.dynamic_slice_in_dim(shard, y * C, C, 1).transpose(1, 0, 2)

    lanes = 128 if rows % 128 == 0 else rows
    tok_all, pos_all, w_qkv, w_out, gate_all, up_all, down_all = gather_start(
        grid, (out_target, out_source), tokens.reshape(rows, width),
        positions.reshape(rows // lanes, lanes), pack, own_pair(qkv_shard), w_output,
        own_pair(hidden_columns(w_gate)), own_pair(hidden_columns(w_up)), w_down,
    )
    x_group = tok_all.reshape(group_tokens, width)
    place = pos_all.reshape(group_tokens)
    packs = w_out[:, :, -8 * C :].reshape(ZA * C, 8 * width)
    ga = packs[:, :n].reshape(1, width).astype(F32)
    gm = packs[:, n : 2 * n].reshape(1, width).astype(F32)
    gq = packs[:, 2 * n : 2 * n + m].reshape(1, HEAD_DIM).astype(F32)
    gk = packs[:, 2 * n + m : 2 * n + 2 * m].reshape(1, HEAD_DIM).astype(F32)
    w_qkv = w_qkv.reshape(width, qkv_width)
    w_out = w_out[:, :, : -8 * C].reshape(-1, width)

    freqs = THETA ** (-(jnp.arange(HALF, dtype=F32) * 2.0 / HEAD_DIM))
    angles = place.astype(F32)[:, None] * freqs
    cosine, sine = jnp.cos(angles), jnp.sin(angles)
    cosine = jnp.concatenate([cosine, cosine], axis=1)
    sine = jnp.concatenate([-sine, sine], axis=1)
    order = (jnp.arange(Y, dtype=jnp.int32) + y) % Y
    nat = jnp.take(block_map.reshape(Y, 2), order, axis=0).reshape(-1)

    def unit_rows(values):
        scale = lax.rsqrt(jnp.mean(values * values, axis=-1, keepdims=True) + EPS)
        return values * scale, scale

    def norm_back(grad, gain, normed, scale):
        grad = grad * gain
        return scale * (grad - normed * jnp.mean(grad * normed, axis=-1, keepdims=True))

    x_unit, _ = unit_rows(x_group.astype(F32))
    h1 = (x_unit * ga).astype(BF)
    lin = dot(h1, w_qkv)
    attended = attend(lin, cosine, sine, gq, gk, nat, seqs, heads, block)
    x_own = tokens.reshape(rows, width).astype(F32)
    x_mid, h2, gate_all, up_all, down_all = join(
        grid, dot(attended, w_out).astype(BF), tokens.reshape(rows, width), gm, gate_all, up_all, down_all
    )
    h2 = h2.reshape(group_tokens, width)
    w_g, w_u = gate_all.reshape(width, -1), up_all.reshape(width, -1)
    side = lax.dynamic_index_in_dim(down_all, a, 1, keepdims=False)
    for k in range(1, A):
        side = send(side, a=1)
        down_all = lax.dynamic_update_slice(down_all, side[:, None], (0, (a - k) % A, 0, 0))
    w_d = down_all.reshape(-1, width)

    mid_unit, mid_scale = unit_rows(x_mid)
    dy = gather_tokens(after((h2,), cotangent.reshape(rows, width)))
    gate = dot(h2, w_g)
    upper = dot(h2, w_u)
    sigmoid = 1.0 / (1.0 + jnp.exp(-gate))
    silu = gate * sigmoid
    hidden = (silu * upper).astype(BF)
    gate_factor = (upper * sigmoid * (1.0 + gate * (1.0 - sigmoid))).astype(BF)
    upper_factor = silu.astype(BF)
    grad_down = dot(hidden, dy, TN).astype(BF)

    def columns_grad(total):
        return shard_of_columns(total)

    def hidden_grad(total):
        whole = shard_of_columns(total).reshape(shard_rows, Y, C, ZA, down_rows)
        return whole.transpose(0, 3, 2, 1, 4).reshape(shard_rows, hidden_units)

    def y_copies(own):
        whole = jnp.zeros((Y,) + own.shape, F32)
        held = own.astype(BF)
        for k in range(Y):
            if k:
                held = send(held, y=1)
            whole = lax.dynamic_update_slice(whole, held[None].astype(F32), ((y - k) % Y, 0, 0))
        return whole.reshape(-1, own.shape[-1])

    def term(partial, i, j):
        at = ((z + i) % Z, (a + j) % A) + (0,) * (partial.ndim - 2)
        return lax.dynamic_slice(partial, at, (1, 1) + partial.shape[2:])[0, 0]

    def meet(*values):
        return lax.optimization_barrier(values)

    class Scatter:
        def __init__(self, partial):
            self.partial = partial
            self.over_a = {}
            self.at = Z - 1
            self.held = None

        def first(self, i):
            return term(self.partial, i, A - 1), dict(a=1)

        def got_first(self, i, held):
            for k in range(1, A):
                total = held.astype(F32) + term(self.partial, i, A - 1 - k).astype(F32)
                if k < A - 1:
                    held = send(total.astype(BF), a=1)
            self.over_a[i] = total
            if i == Z - 1:
                self.total = total

        def hop(self):
            return self.total.astype(BF), dict(z=1)

        def got_hop(self, held):
            self.at -= 1
            self.total = held.astype(F32) + self.over_a[self.at]

    def fly(sends, *values):
        arrays = [v for v, _ in sends]
        out = lax.optimization_barrier((*values, *arrays))
        values, arrays = out[: len(values)], out[len(values) :]
        return values, [send(v, **to) for v, (_, to) in zip(arrays, sends)]

    r_down = Scatter(grad_down.reshape(Z, A, down_rows, width))
    (dy2, w_d2), got = fly([r_down.first(3), r_down.first(2)], dy, w_d)
    d_hidden = dot(dy2, w_d2, NT)
    d_gate = (d_hidden * gate_factor.astype(F32)).astype(BF)
    d_upper = (d_hidden * upper_factor.astype(F32)).astype(BF)
    d_gate, d_upper, *got = meet(d_gate, d_upper, *got)
    r_down.got_first(3, got[0])
    r_down.got_first(2, got[1])
    (d_gate, d_upper), got = fly([r_down.first(1), r_down.first(0), r_down.hop()], d_gate, d_upper)
    d_h2_part = (dot(d_gate, w_g, NT) + dot(d_upper, w_u, NT)).astype(BF)
    d_h2_part, *got = meet(d_h2_part, *got)
    r_down.got_first(1, got[0])
    r_down.got_first(0, got[1])
    r_down.got_hop(got[2])
    parts = d_h2_part.reshape(C, Y, rows, width)
    other = [(parts[1, j], dict(c=1)) for j in range(Y)] if C == 2 else []
    (h2_4, d_gate4), got = fly([*other, r_down.hop()], h2, d_gate)
    grad_gate = dot(h2_4, d_gate4, TN).astype(BF)
    grad_gate, *got = meet(grad_gate, *got)
    r_down.got_hop(got[-1])
    r_gate = Scatter(grad_gate.reshape(Z, A, -1, grad_gate.shape[-1]))
    summed = [parts[0, j].astype(F32) + (got[j].astype(F32) if C == 2 else 0.0) for j in range(Y)]
    (h2_5, d_upper5), got = fly(
        [(summed[Y - 1].astype(BF), dict(y=1)), r_gate.first(3), r_gate.first(2), r_down.hop()], h2, d_upper
    )
    grad_up = dot(h2_5, d_upper5, TN).astype(BF)
    grad_up, *got = meet(grad_up, *got)
    r_gate.got_first(3, got[1])
    r_gate.got_first(2, got[2])
    r_down.got_hop(got[3])
    r_up = Scatter(grad_up.reshape(Z, A, -1, grad_up.shape[-1]))
    d_h2 = got[0].astype(F32) + summed[max(Y - 2, 0)]
    for k in range(2, Y):
        d_h2 = send(d_h2.astype(BF), y=1).astype(F32) + summed[Y - 1 - k]
    sum_mlp = jnp.sum(d_h2 * mid_unit, axis=0)
    d_mid = cotangent.reshape(rows, width).astype(F32) + norm_back(d_h2, gm, mid_unit, mid_scale)
    d_mid_low = d_mid.astype(BF)
    (hidden6, w_d6), got = fly([(d_mid_low, dict(y=1)), r_gate.first(1), r_gate.first(0), r_gate.hop()], hidden, w_d)
    out_part = dot(hidden6, w_d6).astype(BF)
    out_part, *got = meet(out_part, *got)
    r_gate.got_first(1, got[1])
    r_gate.got_first(0, got[2])
    r_gate.got_hop(got[3])
    chunks = [None] * Y
    chunks[0], chunks[Y - 1] = d_mid_low, got[0]
    for k in range(2, Y):
        chunks[Y - k] = send(chunks[Y - k + 1], y=1)
    other = [(chunk, dict(c=1)) for chunk in chunks] if C == 2 else []
    out_parts = out_part.reshape(C, Y, rows, width)
    out_other = [(out_parts[1, j], dict(c=1)) for j in range(Y)] if C == 2 else []
    _, got = fly([*other, *out_other, r_up.first(3), r_gate.hop()])
    got = meet(*got)
    r_up.got_first(3, got[-2])
    r_gate.got_hop(got[-1])
    d_branch = jnp.concatenate([*chunks, *got[: len(other)]], axis=0)
    got = got[len(other) :]
    out_sum = [
        out_parts[0, j].astype(F32) + (got[j].astype(F32) if C == 2 else 0.0) for j in range(Y)
    ]
    (d_branch, w_out8), got = fly(
        [(out_sum[Y - 1].astype(BF), dict(y=1)), r_up.first(2), r_gate.hop(), r_up.hop()], d_branch, w_out
    )
    d_attended = dot(d_branch, w_out8, NT).astype(BF)
    d_lin, sum_query, sum_key = attend_back(
        lin, d_attended, cosine, sine, gq, gk, nat, seqs, heads, block
    )
    d_lin, *got = meet(d_lin, *got)
    out_total = got[0].astype(F32) + out_sum[max(Y - 2, 0)]
    for k in range(2, Y):
        out_total = send(out_total.astype(BF), y=1).astype(F32) + out_sum[Y - 1 - k]
    output = x_mid + out_total
    r_up.got_first(2, got[1])
    r_gate.got_hop(got[2])
    r_up.got_hop(got[3])
    (d_lin, w_qkv9), got = fly([r_up.first(1), r_up.first(0)], d_lin, w_qkv)
    d_h1_part = dot(d_lin, w_qkv9, NT)
    sum_attn = jnp.sum(d_h1_part * x_unit, axis=0)
    d_h1_low, d_lin, *got = meet(d_h1_part.astype(BF), d_lin, *got)
    r_up.got_first(1, got[0])
    r_up.got_first(0, got[1])
    parts = d_h1_low.reshape(C, Y, rows, width)
    other = [(parts[1, j], dict(c=1)) for j in range(Y)] if C == 2 else []
    (h1_10, d_lin), got = fly([*other, r_up.hop()], h1, d_lin)
    grad_qkv = dot(h1_10, d_lin, TN).astype(BF)
    grad_qkv, *got = meet(grad_qkv, *got)
    r_up.got_hop(got[-1])
    summed = [parts[0, j].astype(F32) + (got[j].astype(F32) if C == 2 else 0.0) for j in range(Y)]
    cut = [sum_attn.reshape(ZA * C, n), sum_mlp.reshape(ZA * C, n)]
    cut += [sum_query[0].reshape(ZA * C, m), sum_key[0].reshape(ZA * C, m)]
    sums = jnp.concatenate(cut, axis=1)
    sums = jnp.pad(sums, ((0, 0), (0, 8 * qkv_width - sums.shape[1]))).reshape(ZA * C, 8, qkv_width)
    r_qkv = Scatter(
        jnp.concatenate([grad_qkv.reshape(ZA * C, -1, qkv_width), sums.astype(BF)], axis=1).reshape(
            Z, A, -1, qkv_width
        )
    )
    (attended11, d_branch11), got = fly(
        [(summed[Y - 1].astype(BF), dict(y=1)), r_qkv.first(3), r_qkv.first(2), r_up.hop()], attended, d_branch
    )
    grad_output = dot(attended11, d_branch11, TN).astype(BF)
    grad_output, *got = meet(grad_output, *got)
    d_h1 = got[0].astype(F32) + summed[max(Y - 2, 0)]
    for k in range(2, Y):
        d_h1 = send(d_h1.astype(BF), y=1).astype(F32) + summed[Y - 1 - k]
    r_qkv.got_first(3, got[1])
    r_qkv.got_first(2, got[2])
    r_up.got_hop(got[3])
    r_out = Scatter(grad_output.reshape(Z, A, -1, width))
    own_unit, own_scale = unit_rows(x_own)
    grad_tokens = d_mid + norm_back(d_h1, ga, own_unit, own_scale)
    _, got = fly([r_qkv.first(1), r_qkv.hop(), r_out.first(3), r_out.first(2)])
    got = meet(*got)
    r_qkv.got_first(1, got[0])
    r_qkv.got_hop(got[1])
    r_out.got_first(3, got[2])
    r_out.got_first(2, got[3])
    _, got = fly([r_qkv.first(0), r_qkv.hop(), r_out.hop(), r_out.first(1)])
    got = meet(*got)
    r_qkv.got_first(0, got[0])
    r_qkv.got_hop(got[1])
    r_out.got_first(1, got[3])
    r_out.got_hop(got[2])
    _, got = fly([r_out.first(0), r_qkv.hop(), r_out.hop()])
    got = meet(*got)
    r_out.got_first(0, got[0])
    r_qkv.got_hop(got[1])
    r_out.got_hop(got[2])
    r_out.got_hop(send(*r_out.hop()[:1], z=1))

    g_down = y_copies(r_down.total)
    g_gate = hidden_grad(r_gate.total)
    g_up = hidden_grad(r_up.total)
    whole_qkv = columns_grad(r_qkv.total)
    sums = whole_qkv[shard_rows:].sum((1, 2)).reshape(-1)
    s_attn, s_mlp = sums[:n], sums[n : 2 * n]
    s_query, s_key = sums[2 * n : 2 * n + m], sums[2 * n + m : 2 * n + 2 * m]
    g_qkv = whole_qkv[:shard_rows].reshape(shard_rows, KV_HEADS, (GROUP + 2) * HEAD_DIM)
    g_out = y_copies(grid.permute(r_out.total.astype(BF), out_source))
    g_query = g_qkv[:, :, : GROUP * HEAD_DIM].reshape(shard_rows, -1)
    g_key = g_qkv[:, :, GROUP * HEAD_DIM : (GROUP + 1) * HEAD_DIM].reshape(shard_rows, -1)
    g_value = g_qkv[:, :, (GROUP + 1) * HEAD_DIM :].reshape(shard_rows, -1)

    return (
        output.astype(BF).reshape(tokens.shape), grad_tokens.astype(BF).reshape(tokens.shape),
        g_query, g_key, g_value, g_out, g_gate, g_up, g_down, s_attn, s_mlp, s_query, s_key,
    )


def solution(mesh):
    sharded = P(("dp", "fsdp"), None)
    vector = P(("dp", "fsdp"))
    tokens = P(("dp", "fsdp"), "ctx", None)
    return jax.shard_map(
        functools.partial(on_device, Grid(mesh)),
        mesh=mesh,
        in_specs=(tokens, tokens, P(("dp", "fsdp"), "ctx"), P()) + (sharded,) * 7 + (vector,) * 4,
        out_specs=(tokens, tokens) + (sharded,) * 7 + (vector,) * 4,
        check_vma=False,
    )
```
